128 devices in a mesh: band: 4 (over y_hi, core), tile: 32 (over z, x, y_lo).
Axes of the slice: x: 4, y: 4 (y_hi: 2, y_lo: 2; y = y_hi * 2 + y_lo), z: 4, core: 2. Of those that a mesh axis runs over, the one named last changes fastest.
Arguments:
- traces: float32 [256, 256, 1024], P(None, ('band', 'tile')), may hold values from -6 to 6
- bins: int32 [8], replicated, may hold values from 1 to 31, as said below
Outputs:
- dip_fields: float32 [8, 2, 256, 256, 128], P('band', None, 'tile')
The draws below stay inside these ranges and needn't reach their ends.
Inputs may be any that keep to these rules, and one draw needn't show every extreme that they name: 8 distinct bins, 1 and 31 among them.
All inputs are finite; a program needn't handle non-finite values.
Results may differ from the reference program's by a relative error of at most 0.00018.
Values sent between devices are 32-bit elements; how exact they have to be, the bound alone decides.
A program may use at most 128 MiB of HBM per device.

```python
import math
import jax
import jax.numpy as jnp
from jax import lax

IL_DEV = 8
NT = 1024
NB = 8
WIN = 64
HOP = 8
SEG = 128
R = 3
NF = 128
IL = 256
XL = 256
N_TILE = 32


def draw_bins(key, part):
    inner = jax.random.permutation(key, WIN // 2 - 3)[:NB - 2].astype(jnp.int32) + 2
    return jnp.concatenate([jnp.array([1], jnp.int32), inner, jnp.array([WIN // 2 - 1], jnp.int32)])


def block_scale(rng, dims, cuts, smallest, top_value):
    def one(axis_at, parts):
        heights = jax.random.uniform(jax.random.fold_in(jax.random.fold_in(rng, 6), axis_at), (parts,), jnp.float32, smallest / len(cuts), top_value / len(cuts))
        return jnp.repeat(jnp.exp(heights), dims[axis_at] // parts).reshape((-1,) + (1,) * (len(dims) - axis_at - 1))

    factor_of = one(*cuts[0])
    for cut in cuts[1:]:
        factor_of = factor_of * one(*cut)
    return factor_of


def centred(stream_key, extent, spread, bound, cuts=(), kind=jnp.bfloat16):
    gain = block_scale(stream_key, extent, cuts, -0.22, 0.18) if cuts else 1.0
    drawn = jax.random.normal(stream_key, extent, jnp.float32) * spread * gain
    return jnp.minimum(jnp.maximum(drawn, -bound), bound).astype(kind)


def setup_inputs(seed: int = 0) -> dict:
    key_of = jax.random.split(jax.random.key(seed), 3)
    return {
        "traces": centred(key_of[0], (IL, XL, NT), 1.0, 6.0, ((1, 128),), jnp.float32),
        "bins": draw_bins(jax.random.fold_in(key_of[2], 71), 0),
    }


smooth_sigma = 2.0
tiny_value = 1e-06

def window_kernel(bins):
    band_count = bins.shape[0]
    sample_index = jnp.arange(WIN, dtype=jnp.int32)
    window_taper = 0.5 - 0.5 * jnp.cos(2.0 * math.pi / WIN * sample_index.astype(jnp.float32))
    phase_turns = bins[:, None] * sample_index[None, :] % WIN
    angles = 2.0 * math.pi / WIN * phase_turns.astype(jnp.float32)
    basis_rows = jnp.stack([window_taper * jnp.cos(angles), -window_taper * jnp.sin(angles)])
    frame_count = SEG // HOP
    seg_span = SEG + WIN - HOP
    offset = jnp.arange(seg_span, dtype=jnp.int32)[:, None] - HOP * jnp.arange(frame_count, dtype=jnp.int32)[None, :]
    inside = (offset >= 0) & (offset < WIN)
    picked = jnp.take(basis_rows, jnp.clip(offset, 0, WIN - 1), axis=2)
    kernel_table = jnp.where(inside[None, None], picked, 0.0)
    return jnp.transpose(kernel_table, (2, 0, 1, 3)).reshape(seg_span, 2 * band_count * frame_count)

def band_amplitude(traces, dft_kernel):
    frame_count = SEG // HOP
    seg_span = SEG + WIN - HOP
    block_count = NT // SEG
    band_count = dft_kernel.shape[1] // (2 * frame_count)
    padded = jnp.pad(traces, ((0, 0), (0, 0), (WIN // 2, WIN // 2)))
    pieces = jnp.stack([padded[:, :, block * SEG:block * SEG + seg_span] for block in range(block_count)], axis=2)
    spectra = jnp.dot(pieces, dft_kernel, precision=lax.Precision.HIGHEST, preferred_element_type=jnp.float32)
    spectra = spectra.reshape(traces.shape[0], traces.shape[1], block_count, 2, band_count, frame_count)
    real_part = spectra[:, :, :, 0]
    imag_part = spectra[:, :, :, 1]
    return jnp.sqrt(real_part * real_part + imag_part * imag_part)

def gradients(padded):
    grad_il = (padded[2:, 1:-1, 1:-1] - padded[:-2, 1:-1, 1:-1]) * 0.5
    grad_xl = (padded[1:-1, 2:, 1:-1] - padded[1:-1, :-2, 1:-1]) * 0.5
    grad_time = (padded[1:-1, 1:-1, 2:] - padded[1:-1, 1:-1, :-2]) * 0.5
    return (grad_il, grad_xl, grad_time)

def smooth_axis(field, axis, length):
    weights = [math.exp(-(offset_step * offset_step) / (2.0 * smooth_sigma * smooth_sigma)) for offset_step in range(-R, R + 1)]
    weight_sum = sum(weights)
    result = None
    for position, weight in enumerate(weights):
        section = lax.slice_in_dim(field, position, position + length, axis=axis)
        scaled = weight / weight_sum * section
        result = scaled if result is None else result + scaled
    return result

def smoothed_dips(grad_il, grad_xl, grad_time):
    width = grad_il.shape[0] - 2 * R
    stacked = jnp.stack([grad_il * grad_time, grad_xl * grad_time, grad_time * grad_time])
    along_rows = smooth_axis(stacked, 1, width)
    cross_pad = jnp.pad(along_rows, ((0, 0), (0, 0), (R, R), (0, 0)))
    along_cross = smooth_axis(cross_pad, 2, along_rows.shape[2])
    time_pad = jnp.pad(along_cross, ((0, 0), (0, 0), (0, 0), (R, R)))
    tensor = smooth_axis(time_pad, 3, along_rows.shape[3])
    denominator = tensor[2] + tiny_value
    return jnp.stack([-tensor[0] / denominator, -tensor[1] / denominator])

def band_dips(field):
    grad_il, grad_xl, grad_time = gradients(jnp.pad(field, 1))
    rim_pad = ((R, R), (0, 0), (0, 0))
    return smoothed_dips(jnp.pad(grad_il, rim_pad), jnp.pad(grad_xl, rim_pad), jnp.pad(grad_time, rim_pad))

def reference(traces, bins):
    dft_kernel = window_kernel(bins)
    by_tile = traces.reshape(N_TILE, IL_DEV, XL, NT)
    amplitude = lax.map(lambda block_rows: band_amplitude(block_rows, dft_kernel), by_tile)
    fields = jnp.transpose(amplitude, (4, 0, 1, 2, 3, 5)).reshape(NB, IL, XL, NF)
    return lax.map(band_dips, fields)
```

```python
import functools
import math

import jax
import jax.numpy as jnp
import numpy as np
from jax import lax
from jax.experimental import pallas as pl
from jax.experimental.pallas import tpu as pltpu
from jax.sharding import PartitionSpec as P

WIN = 64
R = 3
NF = 128
SIGMA = 2.0
TINY = 1e-6
MESH = pl.DeviceIdType.MESH
LANES = 128
ROWS = 288
CH = 32
GX = 32


def smooth_weights():
    w = [math.exp(-(k * k) / (2.0 * SIGMA * SIGMA)) for k in range(-R, R + 1)]
    total = sum(w)
    return [v / total for v in w]


def time_matrix():
    w = smooth_weights()
    m = np.zeros((NF, NF), np.float64)
    for lane in range(NF):
        f = (lane + 4) % NF
        for k in range(-R, R + 1):
            if 0 <= f + k < NF:
                m[lane, f + k] = w[k + R]
    hi = m.astype(jnp.bfloat16)
    lo = (m - hi.astype(np.float64)).astype(jnp.bfloat16)
    zero = np.zeros_like(lo)
    return np.concatenate(
        [np.concatenate([hi, lo], axis=1), np.concatenate([hi, zero], axis=1)], axis=0
    )


def split(x):
    hi = x.astype(jnp.bfloat16)
    return hi, (x - hi.astype(jnp.float32)).astype(jnp.bfloat16)


def build_table(bins_ref, wh, wl):
    k = lax.broadcasted_iota(jnp.int32, (256, LANES), 0)
    lane = lax.broadcasted_iota(jnp.int32, (256, LANES), 1)
    group = lane // 16
    bins = jnp.zeros((256, LANES), jnp.int32)
    for b in range(8):
        bins = jnp.where(group == b, bins_ref[b], bins)
    frame = lane % 16
    n = k - 8 * frame
    inside = (n >= 0) & (n < WIN)
    step = 2.0 * math.pi / WIN
    taper = 0.5 - 0.5 * jnp.cos(step * n.astype(jnp.float32))
    angle = step * ((bins * n) & (WIN - 1)).astype(jnp.float32)
    re = jnp.where(inside, taper * jnp.cos(angle), 0.0)
    im = jnp.where(inside, -(taper * jnp.sin(angle)), 0.0)
    keep = (frame < 12) == (k < 128)
    for c, part in enumerate((re, im)):
        cols = slice(c * LANES, (c + 1) * LANES)
        for s, value in enumerate((part, jnp.where(keep, part, 0.0))):
            hi, lo = split(value)
            wh[s, :, cols] = hi
            wl[s, :, cols] = lo


def amplitude_step(c, xv, wh, wl, send):
    group = lax.broadcasted_iota(jnp.int32, (CH, LANES), 1) // 16
    for e in range(2):
        tiles = [
            split(xv[pl.ds(c * (CH * 16) + 2 * t + e, CH, stride=16), :]) for t in range(8)
        ]
        wide = [
            [jnp.concatenate([tiles[s][h], tiles[(s + 1) % 8][h]], axis=1) for s in range(8)]
            for h in range(2)
        ]

        def product(first, last, table):
            hi = jnp.concatenate(wide[0][first:last], axis=0)
            lo = jnp.concatenate(wide[1][first:last], axis=0)
            dot = functools.partial(jnp.dot, preferred_element_type=jnp.float32)
            return dot(hi, wh[table]) + dot(lo, wh[table]) + dot(hi, wl[table])

        spec = jnp.concatenate([product(0, 7, 0), product(7, 8, 1)], axis=0)
        re, im = spec[:, :LANES], spec[:, LANES:]
        amp = jnp.sqrt(re * re + im * im)
        v = [amp[s * CH : (s + 1) * CH] for s in range(8)]
        for d in (4, 2, 1):
            low = (group & d) == 0
            for i in range(8):
                if i & d == 0:
                    a, b = v[i], v[i + d]
                    v[i] = jnp.where(low, a, pltpu.roll(b, 16 * d, axis=1))
                    v[i + d] = jnp.where(low, pltpu.roll(a, LANES - 16 * d, axis=1), b)
        for b in range(8):
            send[b, e, pl.ds(pl.multiple_of(c * CH, CH), CH), :] = v[b]


def products_step(g, recv, q):
    lane = lax.broadcasted_iota(jnp.int32, (8, LANES), 1)
    w = smooth_weights()

    def rows(xl, row):
        return recv[pl.ds((8 * g + xl + 1) * 16 + row, 8, stride=16), :]

    a = [rows(0, r) for r in range(16)]
    p = [[], [], []]
    for r in range(1, 15):
        later = jnp.where(lane == 123, 0.0, pltpu.roll(a[r], LANES - 1, axis=1))
        earlier = jnp.where(lane == 124, 0.0, pltpu.roll(a[r], 1, axis=1))
        gt = later - earlier
        p[0].append((a[r + 1] - a[r - 1]) * gt)
        p[1].append((rows(1, r) - rows(-1, r)) * gt)
        p[2].append(gt * gt)
    for i in range(3):
        for r in range(8):
            s = w[3] * p[i][r + 3]
            for k in range(1, 4):
                s = s + w[3 + k] * (p[i][r + 3 - k] + p[i][r + 3 + k])
            q[i, pl.ds((8 * g + 3) * 8 + r, 8, stride=8), :] = s


def smooth_step(g, q, tmat, out):
    w = smooth_weights()
    sm = []
    for i in range(3):
        load = lambda x: q[i, pl.ds(pl.multiple_of((GX * g + x) * 8, 8), GX * 8), :]
        s = w[3] * load(3)
        for k in range(1, 4):
            s = s + w[3 + k] * (load(3 - k) + load(3 + k))
        sm.append(s)
    hi, lo = split(jnp.concatenate(sm, axis=0))
    t = jnp.dot(
        jnp.concatenate([hi, lo], axis=1), tmat[...], preferred_element_type=jnp.float32
    )
    t = t[:, :LANES] + t[:, LANES:]
    m = GX * 8
    inv = -1.0 / (t[2 * m :] + 4.0 * TINY)
    for i in range(2):
        d = t[i * m : (i + 1) * m] * inv
        for x in range(GX):
            out[i, pl.ds(GX * g + x, 8, stride=256), :] = d[8 * x : 8 * x + 8]


def kernel(
    x_hbm, bins_ref, tmat, out_hbm, xv, wh, wl, send, recv, q, out, in_sem, ssem, rsem, own_sem, osem
):
    band, tile = lax.axis_index("band"), lax.axis_index("tile")
    me = band * 32 + tile
    z, x = tile // 8, (tile // 2) % 4
    y, core = (band // 2) * 2 + tile % 2, band % 2

    def partner(k):
        k = lax.rem(k * 85, 128)
        dc, dz, dx, dy = k // 64, (k // 16) % 4, (k // 4) % 4, k % 4
        z2, x2, y2, c2 = (z + dz) % 4, (x + dx) % 4, (y + dy) % 4, (core + dc) % 2
        return (y2 // 2) * 2 + c2, z2 * 8 + x2 * 2 + y2 % 2

    barrier = pltpu.get_barrier_semaphore()

    def greet(k, carry):
        pl.semaphore_signal(barrier, inc=1, device_id=partner(k), device_id_type=MESH)
        return carry

    load = pltpu.make_async_copy(x_hbm, xv.at[pl.ds(64, 4096)], in_sem)
    load.start()
    lax.fori_loop(1, 128, greet, 0)
    build_table(bins_ref, wh, wl)
    xv[pl.ds(0, 64), :] = jnp.zeros((64, LANES), jnp.float32)
    xv[pl.ds(4160, 16 * ROWS - 4160), :] = jnp.zeros((16 * ROWS - 4160, LANES), jnp.float32)
    for j in range(2):
        recv[j, pl.ds(0, 16), :] = jnp.zeros((16, LANES), jnp.float32)
        recv[j, pl.ds(257 * 16, 16), :] = jnp.zeros((16, LANES), jnp.float32)
    for i in range(3):
        q[i, pl.ds(0, 24), :] = jnp.zeros((24, LANES), jnp.float32)
        q[i, pl.ds(259 * 8, 24), :] = jnp.zeros((24, LANES), jnp.float32)
    load.wait()

    def amp(c, carry):
        amplitude_step(c, xv, wh, wl, send)
        return carry

    lax.fori_loop(0, ROWS // CH, amp, 0)
    pl.semaphore_wait(barrier, 127)

    def chunk(j, e, b2, t2):
        return (
            send.at[b2 * 2 + j, e, pl.ds(pl.multiple_of(t2 * 8, 8), 16)],
            recv.at[j, pl.ds(pl.multiple_of((2 * me + e + 1) * 16, 16), 16)],
        )

    def push(j):
        def body(k, carry):
            b2, t2 = partner(k)
            for e in range(2):
                src, dst = chunk(j, e, b2, t2)
                pltpu.make_async_remote_copy(
                    src, dst, ssem, rsem.at[j], device_id=(b2, t2), device_id_type=MESH
                ).start()
            return carry

        lax.fori_loop(1, 128, body, 0)
        own = []
        for e in range(2):
            src, dst = chunk(j, e, band, tile)
            own.append(pltpu.make_async_copy(src, dst, own_sem.at[j, e]))
            own[-1].start()
        return own

    own = [push(0), push(1)]

    def arrivals(j):
        part = pl.ds(16, 254 * 16)
        return pltpu.make_async_remote_copy(
            recv.at[j, part],
            recv.at[j, part],
            ssem,
            rsem.at[j],
            device_id=(band, lax.rem(tile + 1, 32)),
            device_id_type=MESH,
        )

    results = []
    for j in range(2):
        for copy in own[j]:
            copy.wait()
        arrivals(j).wait_recv()

        def prod(g, carry):
            products_step(g, recv.at[j], q)
            return carry

        def smooth(g, carry):
            smooth_step(g, q, tmat, out.at[j])
            return carry

        lax.fori_loop(0, 32, prod, 0)
        lax.fori_loop(0, 256 // GX, smooth, 0)
        results.append(pltpu.make_async_copy(out.at[j], out_hbm.at[j], osem.at[j]))
        results[-1].start()
    for j in range(2):
        arrivals(j).wait_send()
    for copy in results:
        copy.wait()


def local(traces, bins):
    x = traces.reshape(256, 2, 8, LANES).transpose(0, 2, 1, 3).reshape(4096, LANES)
    tmat = jnp.asarray(time_matrix())
    f32 = jnp.float32
    out = pl.pallas_call(
        kernel,
        out_shape=jax.ShapeDtypeStruct((2, 2, 2048, LANES), f32),
        in_specs=[
            pl.BlockSpec(memory_space=pl.ANY),
            pl.BlockSpec(memory_space=pltpu.SMEM),
            pl.BlockSpec(memory_space=pltpu.VMEM),
        ],
        out_specs=pl.BlockSpec(memory_space=pl.ANY),
        scratch_shapes=[
            pltpu.VMEM((16 * ROWS, LANES), f32),
            pltpu.VMEM((2, 256, 256), jnp.bfloat16),
            pltpu.VMEM((2, 256, 256), jnp.bfloat16),
            pltpu.VMEM((8, 2, ROWS, LANES), f32),
            pltpu.VMEM((2, 258 * 16, LANES), f32),
            pltpu.VMEM((3, 262 * 8, LANES), f32),
            pltpu.VMEM((2, 2, 2048, LANES), f32),
            pltpu.SemaphoreType.DMA,
            pltpu.SemaphoreType.DMA,
            pltpu.SemaphoreType.DMA((2,)),
            pltpu.SemaphoreType.DMA((2, 2)),
            pltpu.SemaphoreType.DMA((2,)),
        ],
        compiler_params=pltpu.CompilerParams(
            collective_id=0, has_side_effects=True, vmem_limit_bytes=60 << 20
        ),
        name="spectral_dips",
    )(x, bins, tmat)
    return out.reshape(2, 2, 8, 256, NF)


def solution(mesh):
    in_specs = (P(None, ("band", "tile"), None), P())
    out_specs = P("band", None, "tile", None, None)
    return jax.shard_map(local, mesh=mesh, in_specs=in_specs, out_specs=out_specs, check_vma=False)
```

```python
import functools
import math

import jax
import jax.numpy as jnp
from jax import lax
from jax.experimental import pallas as pl
from jax.experimental.pallas import tpu as pltpu
from jax.sharding import PartitionSpec as P

WIN = 64
R = 3
NF = 128
SIGMA = 2.0
TINY = 1e-6
MESH = pl.DeviceIdType.MESH
LANES = 128
TILES = 4
CH = 8 * TILES + 8
GX = 32


def smooth_weights():
    w = [math.exp(-(k * k) / (2.0 * SIGMA * SIGMA)) for k in range(-R, R + 1)]
    total = sum(w)
    return [v / total for v in w]


def split(x):
    hi = x.astype(jnp.bfloat16)
    return hi, (x - hi.astype(jnp.float32)).astype(jnp.bfloat16)


def build_time_matrix(tmat):
    lane = lax.broadcasted_iota(jnp.int32, (NF, NF), 0)
    frame = lax.broadcasted_iota(jnp.int32, (NF, NF), 1)
    away = jnp.abs(((lane + 4) & (NF - 1)) - frame)
    value = jnp.zeros((NF, NF), jnp.float32)
    for k, weight in enumerate(smooth_weights()[R:]):
        value = jnp.where(away == k, weight, value)
    hi, lo = split(value)
    tmat[pl.ds(0, NF), pl.ds(0, NF)] = hi
    tmat[pl.ds(NF, NF), pl.ds(0, NF)] = hi
    tmat[pl.ds(0, NF), pl.ds(NF, NF)] = lo
    tmat[pl.ds(NF, NF), pl.ds(NF, NF)] = jnp.zeros((NF, NF), jnp.bfloat16)


def build_table(bins_ref, wh, wl):
    k = lax.broadcasted_iota(jnp.int32, (256, LANES), 0)
    lane = lax.broadcasted_iota(jnp.int32, (256, LANES), 1)
    group = lane // 16
    bins = jnp.zeros((256, LANES), jnp.int32)
    for b in range(8):
        bins = jnp.where(group == b, bins_ref[b], bins)
    frame = lane % 16
    n = k - 8 * frame
    inside = (n >= 0) & (n < WIN)
    step = 2.0 * math.pi / WIN
    taper = 0.5 - 0.5 * jnp.cos(step * n.astype(jnp.float32))
    angle = step * ((bins * n) & (WIN - 1)).astype(jnp.float32)
    re = jnp.where(inside, taper * jnp.cos(angle), 0.0)
    im = jnp.where(inside, -(taper * jnp.sin(angle)), 0.0)
    keep = (frame < 12) == (k < 128)
    for c, part in enumerate((re, im)):
        cols = slice(c * LANES, (c + 1) * LANES)
        for s, value in enumerate((part, jnp.where(keep, part, 0.0))):
            hi, lo = split(value)
            wh[s, :, cols] = hi
            wl[s, :, cols] = lo


def amplitude_step(c, xv, wh, wl, send):
    group = lax.broadcasted_iota(jnp.int32, (CH, LANES), 1) // 16
    tiles = [
        [xv[pl.ds(c * (TILES * 128) + 2 * t + e, CH, stride=16), :] for t in range(8)]
        for e in range(2)
    ]

    def product(segments, table):
        hi, lo = split(
            jnp.concatenate(
                [
                    jnp.concatenate([tiles[e][s], tiles[e][(s + 1) % 8]], axis=1)
                    for e in range(2)
                    for s in segments
                ],
                axis=0,
            )
        )
        dot = functools.partial(jnp.dot, preferred_element_type=jnp.float32)
        spec = dot(hi, wh[table]) + dot(lo, wh[table]) + dot(hi, wl[table])
        re, im = spec[:, :LANES], spec[:, LANES:]
        amp = jnp.sqrt(re * re + im * im)
        n = len(segments)
        return [
            [amp[(e * n + s) * CH : (e * n + s + 1) * CH] for s in range(n)] for e in range(2)
        ]

    first, last = product(range(7), 0), product([7], 1)
    for e in range(2):
        v = first[e] + last[e]
        for d in (4, 2, 1):
            low = (group & d) == 0
            for i in range(8):
                if i & d == 0:
                    a, b = v[i], v[i + d]
                    v[i] = jnp.where(low, a, pltpu.roll(b, 16 * d, axis=1))
                    v[i + d] = jnp.where(low, pltpu.roll(a, LANES - 16 * d, axis=1), b)
        for b in range(8):
            send[c, b, e] = v[b]


def products_step(g, recv, q):
    lane = lax.broadcasted_iota(jnp.int32, (8, LANES), 1)
    w = smooth_weights()

    def rows(xl, row):
        return recv[pl.ds((8 * g + xl + 1) * 16 + row, 8, stride=16), :]

    a = [rows(0, r) for r in range(16)]
    p = [[], [], []]
    for r in range(1, 15):
        later = jnp.where(lane == 123, 0.0, pltpu.roll(a[r], LANES - 1, axis=1))
        earlier = jnp.where(lane == 124, 0.0, pltpu.roll(a[r], 1, axis=1))
        gt = later - earlier
        p[0].append((a[r + 1] - a[r - 1]) * gt)
        p[1].append((rows(1, r) - rows(-1, r)) * gt)
        p[2].append(gt * gt)
    for i in range(3):
        for r in range(8):
            s = w[3] * p[i][r + 3]
            for k in range(1, 4):
                s = s + w[3 + k] * (p[i][r + 3 - k] + p[i][r + 3 + k])
            q[i, pl.ds((8 * g + 3) * 8 + r, 8, stride=8), :] = s


def smooth_step(g, q, tmat, out):
    w = smooth_weights()
    sm = []
    for i in range(3):
        load = lambda x: q[i, pl.ds(pl.multiple_of((GX * g + x) * 8, 8), GX * 8), :]
        s = w[3] * load(3)
        for k in range(1, 4):
            s = s + w[3 + k] * (load(3 - k) + load(3 + k))
        sm.append(s)
    hi, lo = split(jnp.concatenate(sm, axis=0))
    t = jnp.dot(
        jnp.concatenate([hi, lo], axis=1), tmat[...], preferred_element_type=jnp.float32
    )
    t = t[:, :LANES] + t[:, LANES:]
    m = GX * 8
    inv = -1.0 / (t[2 * m :] + 4.0 * TINY)
    for i in range(2):
        d = t[i * m : (i + 1) * m] * inv
        for x in range(GX):
            out[i, pl.ds(GX * g + x, 8, stride=256), :] = d[8 * x : 8 * x + 8]


def exchange_kernel(
    x_hbm, bins_hbm, dip, last, xv, bins_ref, wh, wl, send, recv, q, tmat, in_sem, ssem, rsem, own_sem
):
    band, tile = lax.axis_index("band"), lax.axis_index("tile")
    me = band * 32 + tile
    home = tile >> 2

    def partner(k):
        other = me ^ k
        return other >> 5, other & 31

    barrier = pltpu.get_barrier_semaphore()

    def greet(k, carry):
        pl.semaphore_signal(barrier, inc=1, device_id=partner(k), device_id_type=MESH)
        return carry

    load = pltpu.make_async_copy(x_hbm, xv.at[pl.ds(64, 4096)], in_sem.at[0])
    load.start()
    load_bins = pltpu.make_async_copy(bins_hbm, bins_ref, in_sem.at[1])
    load_bins.start()
    lax.fori_loop(1, 128, greet, 0)
    load_bins.wait()
    build_table(bins_ref, wh, wl)
    build_time_matrix(tmat)
    for start in (0, 4160):
        xv[pl.ds(start, 64), :] = jnp.zeros((64, LANES), jnp.float32)
    for start in (0, 257 * 16):
        recv[pl.ds(start, 16), :] = jnp.zeros((16, LANES), jnp.float32)
        last[pl.ds(start, 16), :] = jnp.zeros((16, LANES), jnp.float32)
    clear_rim(q)
    load.wait()

    def step_of(half, m):
        return (m << 1) | ((m ^ (m >> 1) ^ half) & 1)

    def form(half):
        def body(m, carry):
            amplitude_step(home ^ step_of(half, m), xv, wh, wl, send)
            return carry

        lax.fori_loop(0, 4, body, 0)

    def chunk(j, e, b2, t2):
        source = send.at[t2 >> 2, b2 * 2 + j, e, pl.ds(pl.multiple_of((t2 & 3) * 8, 8), 16)]
        place = pl.ds(pl.multiple_of((2 * me + e + 1) * 16, 16), 16)
        return source, (recv, last)[j].at[place]

    def push(j, k):
        b2, t2 = partner(k)
        for e in range(2):
            src, dst = chunk(j, e, b2, t2)
            pltpu.make_async_remote_copy(
                src, dst, ssem.at[j], rsem.at[j], device_id=(b2, t2), device_id_type=MESH
            ).start()

    def push_half(half):
        def body(n, carry):
            n = (n * 5) & 63
            push(0, ((n & 48) << 1) | (step_of(half, (n >> 2) & 3) << 2) | (n & 3))
            return carry

        lax.fori_loop(1 - half, 64, body, 0)

    def keep(j):
        own = []
        for e in range(2):
            src, dst = chunk(j, e, band, tile)
            own.append(pltpu.make_async_copy(src, dst, own_sem.at[j, e]))
            own[-1].start()
        return own

    form(0)
    pl.semaphore_wait(barrier, 127)
    own = keep(0)
    push_half(0)
    form(1)
    push_half(1)

    def arrivals(j):
        part = (recv, last)[j].at[pl.ds(16, 254 * 16)]
        return pltpu.make_async_remote_copy(
            part,
            part,
            ssem.at[j],
            rsem.at[j],
            device_id=(band, tile ^ 1),
            device_id_type=MESH,
        )

    def second(k, carry):
        push(1, (k * 75) & 127)
        return carry

    lax.fori_loop(1, 128, second, 0)
    own += keep(1)
    for copy in own[:2]:
        copy.wait()
    arrivals(0).wait_recv()

    def prod(g, carry):
        products_step(g, recv, q)
        return carry

    def smooth(g, carry):
        smooth_step(g, q, tmat, dip)
        return carry

    lax.fori_loop(0, 32, prod, 0)
    lax.fori_loop(0, 256 // GX, smooth, 0)
    for copy in own[2:]:
        copy.wait()
    arrivals(1).wait_recv()
    for j in range(2):
        arrivals(j).wait_send()


def clear_rim(q):
    for i in range(3):
        for start in (0, 259 * 8):
            q[i, pl.ds(start, 24), :] = jnp.zeros((24, LANES), jnp.float32)


def dips_kernel(dip, last, out_hbm, q, out, tmat, sems):
    give = pltpu.make_async_copy(dip, out_hbm.at[0], sems.at[0])
    give.start()
    clear_rim(q)
    build_time_matrix(tmat)

    def prod(g, carry):
        products_step(g, last, q)
        return carry

    def smooth(g, carry):
        smooth_step(g, q, tmat, out)
        return carry

    lax.fori_loop(0, 32, prod, 0)
    lax.fori_loop(0, 256 // GX, smooth, 0)
    result = pltpu.make_async_copy(out, out_hbm.at[1], sems.at[1])
    result.start()
    result.wait()
    give.wait()


def local(traces, bins):
    x = traces.reshape(256, 2, 8, LANES).transpose(0, 2, 1, 3).reshape(4096, LANES)
    x = pltpu.with_memory_space_constraint(x, pltpu.HBM)
    bins = pltpu.with_memory_space_constraint(bins, pltpu.HBM)
    f32 = jnp.float32
    dma = pltpu.SemaphoreType.DMA
    anywhere = pl.BlockSpec(memory_space=pl.ANY)
    in_vmem = pl.BlockSpec(memory_space=pltpu.VMEM)
    field = pltpu.VMEM((2, 2048, LANES), f32)
    window = pltpu.VMEM((258 * 16, LANES), f32)
    tensor = pltpu.VMEM((3, 262 * 8, LANES), f32)
    matrix = pltpu.VMEM((2 * NF, 2 * NF), jnp.bfloat16)
    dip, last = pl.pallas_call(
        exchange_kernel,
        out_shape=(
            jax.ShapeDtypeStruct((2, 2048, LANES), f32),
            jax.ShapeDtypeStruct((258 * 16, LANES), f32),
        ),
        in_specs=[pl.BlockSpec(memory_space=pltpu.HBM)] * 2,
        out_specs=(in_vmem, in_vmem),
        scratch_shapes=[
            pltpu.VMEM((264 * 16, LANES), f32),
            pltpu.SMEM((8,), jnp.int32),
            pltpu.VMEM((2, 256, 256), jnp.bfloat16),
            pltpu.VMEM((2, 256, 256), jnp.bfloat16),
            pltpu.VMEM((8, 8, 2, CH, LANES), f32),
            window,
            tensor,
            matrix,
            dma((2,)),
            dma((2,)),
            dma((2,)),
            dma((2, 2)),
        ],
        compiler_params=pltpu.CompilerParams(
            collective_id=0, has_side_effects=True, vmem_limit_bytes=40 << 20
        ),
        name="transform_exchange",
    )(x, bins)
    out = pl.pallas_call(
        dips_kernel,
        out_shape=jax.ShapeDtypeStruct((2, 2, 2048, LANES), f32),
        in_specs=[in_vmem, in_vmem],
        out_specs=anywhere,
        scratch_shapes=[tensor, field, matrix, dma((2,))],
        compiler_params=pltpu.CompilerParams(vmem_limit_bytes=32 << 20),
        name="last_band_dips",
    )(dip, last)
    return out.reshape(2, 2, 8, 256, NF)


def solution(mesh):
    in_specs = (P(None, ("band", "tile"), None), P())
    out_specs = P("band", None, "tile", None, None)
    return jax.shard_map(local, mesh=mesh, in_specs=in_specs, out_specs=out_specs, check_vma=False)
```

```python
import functools
import math

import jax
import jax.numpy as jnp
from jax import lax
from jax.experimental import pallas as pl
from jax.experimental.pallas import tpu as pltpu
from jax.sharding import PartitionSpec as P

WIN = 64
R = 3
NF = 128
SIGMA = 2.0
TINY = 1e-6
MESH = pl.DeviceIdType.MESH
LANES = 128
TILES = 4
CH = 8 * TILES + 8
PX = 8
GX = 64


def smooth_weights():
    w = [math.exp(-(k * k) / (2.0 * SIGMA * SIGMA)) for k in range(-R, R + 1)]
    total = sum(w)
    return [v / total for v in w]


def side_weights():
    w = smooth_weights()
    return [w[R + k] / w[R] for k in range(1, R + 1)]


def split(x):
    hi = x.astype(jnp.bfloat16)
    return hi, (x - hi.astype(jnp.float32)).astype(jnp.bfloat16)


def build_time_matrix(tmat):
    lane = lax.broadcasted_iota(jnp.int32, (NF, NF), 0)
    frame = lax.broadcasted_iota(jnp.int32, (NF, NF), 1)
    away = jnp.abs(((lane + 4) & (NF - 1)) - frame)
    value = jnp.zeros((NF, NF), jnp.float32)
    w = smooth_weights()
    for k in range(R + 1):
        value = jnp.where(away == k, w[R + k] * w[R] * w[R], value)
    hi, lo = split(value)
    tmat[pl.ds(0, NF), pl.ds(0, NF)] = hi
    tmat[pl.ds(NF, NF), pl.ds(0, NF)] = hi
    tmat[pl.ds(0, NF), pl.ds(NF, NF)] = lo
    tmat[pl.ds(NF, NF), pl.ds(NF, NF)] = jnp.zeros((NF, NF), jnp.bfloat16)


def build_table(bins_ref, wh, wl):
    k = lax.broadcasted_iota(jnp.int32, (256, LANES), 0)
    lane = lax.broadcasted_iota(jnp.int32, (256, LANES), 1)
    group = lane // 16
    bins = jnp.zeros((256, LANES), jnp.int32)
    for b in range(8):
        bins = jnp.where(group == b, bins_ref[b], bins)
    frame = lane % 16
    n = k - 8 * frame
    inside = (n >= 0) & (n < WIN)
    step = 2.0 * math.pi / WIN
    taper = 0.5 - 0.5 * jnp.cos(step * n.astype(jnp.float32))
    angle = step * ((bins * n) & (WIN - 1)).astype(jnp.float32)
    re = jnp.where(inside, taper * jnp.cos(angle), 0.0)
    im = jnp.where(inside, -(taper * jnp.sin(angle)), 0.0)
    keep = (frame < 12) == (k < 128)
    for c, part in enumerate((re, im)):
        cols = slice(c * LANES, (c + 1) * LANES)
        for s, value in enumerate((part, jnp.where(keep, part, 0.0))):
            hi, lo = split(value)
            wh[s, :, cols] = hi
            wl[s, :, cols] = lo


def amplitude_step(c, xv, wh, wl, send):
    group = lax.broadcasted_iota(jnp.int32, (CH, LANES), 1) // 16
    tiles = [
        [xv[pl.ds(c * (TILES * 128) + 2 * t + e, CH, stride=16), :] for t in range(8)]
        for e in range(2)
    ]

    def product(segments, table):
        hi, lo = split(
            jnp.concatenate(
                [
                    jnp.concatenate([tiles[e][s], tiles[e][(s + 1) % 8]], axis=1)
                    for e in range(2)
                    for s in segments
                ],
                axis=0,
            )
        )
        dot = functools.partial(jnp.dot, preferred_element_type=jnp.float32)
        spec = dot(hi, wh[table]) + dot(lo, wh[table]) + dot(hi, wl[table])
        re, im = spec[:, :LANES], spec[:, LANES:]
        amp = jnp.sqrt(re * re + im * im)
        n = len(segments)
        return [
            [amp[(e * n + s) * CH : (e * n + s + 1) * CH] for s in range(n)] for e in range(2)
        ]

    first, last = product(range(7), 0), product([7], 1)
    for e in range(2):
        v = first[e] + last[e]
        for d in (4, 2, 1):
            low = (group & d) == 0
            for i in range(8):
                if i & d == 0:
                    a, b = v[i], v[i + d]
                    v[i] = jnp.where(low, a, pltpu.roll(b, 16 * d, axis=1))
                    v[i + d] = jnp.where(low, pltpu.roll(a, LANES - 16 * d, axis=1), b)
        for b in range(8):
            send[c, b, e] = v[b]


def products_step(g, recv, taps, slot):
    lane = lax.broadcasted_iota(jnp.int32, (8, LANES), 1)

    def rows(xl, first):
        return recv[pl.ds((PX * g + xl + 1) * 16 + first, 8), :]

    centre = [[rows(x, first) for first in (1, 7)] for x in range(-1, PX + 1)]
    for x in range(PX):
        for half, first in enumerate((1, 7)):
            a = centre[x + 1][half]
            later = jnp.where(lane == 123, 0.0, pltpu.roll(a, LANES - 1, axis=1))
            earlier = jnp.where(lane == 124, 0.0, pltpu.roll(a, 1, axis=1))
            gt = later - earlier
            gi = rows(x, first + 1) - rows(x, first - 1)
            gx = centre[x + 2][half] - centre[x][half]
            for i, p in enumerate((gi * gt, gx * gt, gt * gt)):
                taps[slot, i, x, pl.ds(first - 1, 8), :] = p


def rows_step(g, taps, slot, q):
    w = side_weights()
    for x in range(PX):
        for i in range(3):
            tap = [taps[slot, i, x, pl.ds(k, 8), :] for k in range(7)]
            s = tap[3]
            for k in range(1, 4):
                s = s + w[k - 1] * (tap[3 - k] + tap[3 + k])
            q[i, pl.ds(pl.multiple_of((PX * g + x + 3) * 8, 8), 8), :] = s


def tensor_rows(recv, q, taps):
    last = 256 // PX - 1
    products_step(0, recv, taps, 0)

    def pair(h, carry):
        rows_step(2 * h, taps, 0, q)
        products_step(2 * h + 1, recv, taps, 1)
        rows_step(2 * h + 1, taps, 1, q)
        products_step(2 * h + 2, recv, taps, 0)
        return carry

    lax.fori_loop(0, last // 2, pair, 0)
    rows_step(last - 1, taps, 0, q)
    products_step(last, recv, taps, 1)
    rows_step(last, taps, 1, q)


def smooth_step(g, q, tmat, turn, out):
    w = side_weights()
    sm = []
    for i in range(3):
        load = lambda x: q[i, pl.ds(pl.multiple_of((GX * g + x) * 8, 8), GX * 8), :]
        s = load(3)
        for k in range(1, 4):
            s = s + w[k - 1] * (load(3 - k) + load(3 + k))
        sm.append(s)
    hi, lo = split(jnp.concatenate(sm, axis=0))
    t = jnp.dot(
        jnp.concatenate([hi, lo], axis=1), tmat[...], preferred_element_type=jnp.float32
    )
    t = t[:, :LANES] + t[:, LANES:]
    m = GX * 8
    inv = -1.0 / (t[2 * m :] + 4.0 * TINY)
    for i in range(2):
        d = t[i * m : (i + 1) * m] * inv
        for x in range(GX):
            turn[i, x // 8, pl.ds(x % 8, 8, stride=8), :] = d[8 * x : 8 * x + 8]
        for block in range(GX // 8):
            for row in range(8):
                place = pl.ds(pl.multiple_of(row * 256 + GX * g + 8 * block, 8), 8)
                out[i, place, :] = turn[i, block, pl.ds(8 * row, 8), :]


def clear_rim(q):
    for i in range(3):
        for start in (0, 259 * 8):
            q[i, pl.ds(start, 24), :] = jnp.zeros((24, LANES), jnp.float32)


def exchange_kernel(
    x_hbm, bins_hbm, dip, last, xv, bins_ref, wh, wl, send, recv, q, tmat, taps, turn, in_sem, ssem, rsem, own_sem
):
    band, tile = lax.axis_index("band"), lax.axis_index("tile")
    me = band * 32 + tile
    home = tile >> 2

    def partner(k):
        other = me ^ k
        return other >> 5, other & 31

    barrier = pltpu.get_barrier_semaphore()

    def greet(k, carry):
        pl.semaphore_signal(barrier, inc=1, device_id=partner(k), device_id_type=MESH)
        return carry

    load = pltpu.make_async_copy(x_hbm, xv.at[pl.ds(64, 4096)], in_sem.at[0])
    load.start()
    load_bins = pltpu.make_async_copy(bins_hbm, bins_ref, in_sem.at[1])
    load_bins.start()
    lax.fori_loop(1, 128, greet, 0)
    load_bins.wait()
    build_table(bins_ref, wh, wl)
    build_time_matrix(tmat)
    for start in (0, 4160):
        xv[pl.ds(start, 64), :] = jnp.zeros((64, LANES), jnp.float32)
    for start in (0, 257 * 16):
        recv[pl.ds(start, 16), :] = jnp.zeros((16, LANES), jnp.float32)
        last[pl.ds(start, 16), :] = jnp.zeros((16, LANES), jnp.float32)
    clear_rim(q)
    load.wait()

    def step_of(half, m):
        return (m << 1) | ((m ^ (m >> 1) ^ half) & 1)

    def form(half):
        def body(m, carry):
            amplitude_step(home ^ step_of(half, m), xv, wh, wl, send)
            return carry

        lax.fori_loop(0, 4, body, 0)

    def chunk(j, e, b2, t2):
        source = send.at[t2 >> 2, b2 * 2 + j, e, pl.ds(pl.multiple_of((t2 & 3) * 8, 8), 16)]
        place = pl.ds(pl.multiple_of((2 * me + e + 1) * 16, 16), 16)
        return source, (recv, last)[j].at[place]

    def push(j, k):
        b2, t2 = partner(k)
        for e in range(2):
            src, dst = chunk(j, e, b2, t2)
            pltpu.make_async_remote_copy(
                src, dst, ssem.at[j], rsem.at[j], device_id=(b2, t2), device_id_type=MESH
            ).start()

    def push_half(half):
        def body(n, carry):
            n = (n * 5) & 63
            push(0, ((n & 48) << 1) | (step_of(half, (n >> 2) & 3) << 2) | (n & 3))
            return carry

        lax.fori_loop(1 - half, 64, body, 0)

    def keep(j):
        own = []
        for e in range(2):
            src, dst = chunk(j, e, band, tile)
            own.append(pltpu.make_async_copy(src, dst, own_sem.at[j, e]))
            own[-1].start()
        return own

    form(0)
    pl.semaphore_wait(barrier, 127)
    own = keep(0)
    push_half(0)
    form(1)
    push_half(1)

    def arrivals(j):
        part = (recv, last)[j].at[pl.ds(16, 254 * 16)]
        return pltpu.make_async_remote_copy(
            part,
            part,
            ssem.at[j],
            rsem.at[j],
            device_id=(band, tile ^ 1),
            device_id_type=MESH,
        )

    def second(k, carry):
        push(1, (k * 75) & 127)
        return carry

    lax.fori_loop(1, 128, second, 0)
    own += keep(1)
    for copy in own[:2]:
        copy.wait()
    arrivals(0).wait_recv()

    def smooth(g, carry):
        smooth_step(g, q, tmat, turn, dip)
        return carry

    tensor_rows(recv, q, taps)
    lax.fori_loop(0, 256 // GX, smooth, 0)
    for copy in own[2:]:
        copy.wait()
    arrivals(1).wait_recv()
    for j in range(2):
        arrivals(j).wait_send()


def dips_kernel(dip, last, out_hbm, q, out, tmat, taps, turn, sems, osems):
    give = pltpu.make_async_copy(dip, out_hbm.at[0], sems.at[0])
    give.start()
    clear_rim(q)
    build_time_matrix(tmat)

    def result(i, g):
        return [
            pltpu.make_async_copy(
                out.at[i, pl.ds(pl.multiple_of(256 * row + GX * g, GX), GX)],
                out_hbm.at[1, i, pl.ds(pl.multiple_of(256 * row + GX * g, GX), GX)],
                osems.at[g],
            )
            for row in range(8)
        ]

    def smooth(g, carry):
        smooth_step(g, q, tmat, turn, out)
        for i in range(2):
            for copy in result(i, g):
                copy.start()
        return carry

    tensor_rows(last, q, taps)
    lax.fori_loop(0, 256 // GX, smooth, 0)

    def drain(g, carry):
        for i in range(2):
            pltpu.make_async_copy(
                out.at[i, pl.ds(0, 8 * GX)], out_hbm.at[1, i, pl.ds(0, 8 * GX)], osems.at[g]
            ).wait()
        return carry

    lax.fori_loop(0, 256 // GX, drain, 0)
    give.wait()


def local(traces, bins):
    x = traces.reshape(256, 2, 8, LANES).transpose(0, 2, 1, 3).reshape(4096, LANES)
    x = pltpu.with_memory_space_constraint(x, pltpu.HBM)
    bins = pltpu.with_memory_space_constraint(bins, pltpu.HBM)
    f32 = jnp.float32
    dma = pltpu.SemaphoreType.DMA
    anywhere = pl.BlockSpec(memory_space=pl.ANY)
    in_vmem = pl.BlockSpec(memory_space=pltpu.VMEM)
    field = pltpu.VMEM((2, 2048, LANES), f32)
    window = pltpu.VMEM((258 * 16, LANES), f32)
    tensor = pltpu.VMEM((3, 262 * 8, LANES), f32)
    matrix = pltpu.VMEM((2 * NF, 2 * NF), jnp.bfloat16)
    tap_rows = pltpu.VMEM((2, 3, PX, 16, LANES), f32)
    turned = pltpu.VMEM((2, GX // 8, 64, LANES), f32)
    dip, last = pl.pallas_call(
        exchange_kernel,
        out_shape=(
            jax.ShapeDtypeStruct((2, 2048, LANES), f32),
            jax.ShapeDtypeStruct((258 * 16, LANES), f32),
        ),
        in_specs=[pl.BlockSpec(memory_space=pltpu.HBM)] * 2,
        out_specs=(in_vmem, in_vmem),
        scratch_shapes=[
            pltpu.VMEM((264 * 16, LANES), f32),
            pltpu.SMEM((8,), jnp.int32),
            pltpu.VMEM((2, 256, 256), jnp.bfloat16),
            pltpu.VMEM((2, 256, 256), jnp.bfloat16),
            pltpu.VMEM((8, 8, 2, CH, LANES), f32),
            window,
            tensor,
            matrix,
            tap_rows,
            turned,
            dma((2,)),
            dma((2,)),
            dma((2,)),
            dma((2, 2)),
        ],
        compiler_params=pltpu.CompilerParams(
            collective_id=0, has_side_effects=True, vmem_limit_bytes=40 << 20
        ),
        name="transform_exchange",
    )(x, bins)
    out = pl.pallas_call(
        dips_kernel,
        out_shape=jax.ShapeDtypeStruct((2, 2, 2048, LANES), f32),
        in_specs=[in_vmem, in_vmem],
        out_specs=anywhere,
        scratch_shapes=[tensor, field, matrix, tap_rows, turned, dma((2,)), dma((8,))],
        compiler_params=pltpu.CompilerParams(vmem_limit_bytes=32 << 20),
        name="last_band_dips",
    )(dip, last)
    return out.reshape(2, 2, 8, 256, NF)


def solution(mesh):
    in_specs = (P(None, ("band", "tile"), None), P())
    out_specs = P("band", None, "tile", None, None)
    return jax.shard_map(local, mesh=mesh, in_specs=in_specs, out_specs=out_specs, check_vma=False)
```

```python
import functools
import math

import jax
import jax.numpy as jnp
from jax import lax
from jax.experimental import pallas as pl
from jax.experimental.pallas import tpu as pltpu
from jax.sharding import PartitionSpec as P

WIN = 64
R = 3
NF = 128
SIGMA = 2.0
TINY = 1e-6
MESH = pl.DeviceIdType.MESH
LANES = 128
TILES = 4
CH = 8 * TILES + 8
PX = 8
GX = 64


def smooth_weights():
    w = [math.exp(-(k * k) / (2.0 * SIGMA * SIGMA)) for k in range(-R, R + 1)]
    total = sum(w)
    return [v / total for v in w]


def side_weights():
    w = smooth_weights()
    return [w[R + k] / w[R] for k in range(1, R + 1)]


def split(x):
    hi = x.astype(jnp.bfloat16)
    return hi, (x - hi.astype(jnp.float32)).astype(jnp.bfloat16)


def build_time_matrix(tmat):
    lane = lax.broadcasted_iota(jnp.int32, (NF, NF), 0)
    frame = lax.broadcasted_iota(jnp.int32, (NF, NF), 1)
    away = jnp.abs(((lane + 4) & (NF - 1)) - frame)
    value = jnp.zeros((NF, NF), jnp.float32)
    w = smooth_weights()
    for k in range(R + 1):
        value = jnp.where(away == k, w[R + k] * w[R] * w[R], value)
    hi, lo = split(value)
    tmat[pl.ds(0, NF), pl.ds(0, NF)] = hi
    tmat[pl.ds(NF, NF), pl.ds(0, NF)] = hi
    tmat[pl.ds(0, NF), pl.ds(NF, NF)] = lo
    tmat[pl.ds(NF, NF), pl.ds(NF, NF)] = jnp.zeros((NF, NF), jnp.bfloat16)


def build_table(bins_ref, wh, wl):
    k = lax.broadcasted_iota(jnp.int32, (256, LANES), 0)
    lane = lax.broadcasted_iota(jnp.int32, (256, LANES), 1)
    group = lane // 16
    bins = jnp.zeros((256, LANES), jnp.int32)
    for b in range(8):
        bins = jnp.where(group == b, bins_ref[b], bins)
    frame = lane % 16
    n = k - 8 * frame
    inside = (n >= 0) & (n < WIN)
    step = 2.0 * math.pi / WIN
    taper = 0.5 - 0.5 * jnp.cos(step * n.astype(jnp.float32))
    angle = step * ((bins * n) & (WIN - 1)).astype(jnp.float32)
    re = jnp.where(inside, taper * jnp.cos(angle), 0.0)
    im = jnp.where(inside, -(taper * jnp.sin(angle)), 0.0)
    keep = (frame < 12) == (k < 128)
    for c, part in enumerate((re, im)):
        cols = slice(c * LANES, (c + 1) * LANES)
        for s, value in enumerate((part, jnp.where(keep, part, 0.0))):
            hi, lo = split(value)
            wh[s, :, cols] = hi
            wl[s, :, cols] = lo


def amplitude_step(c, xv, wh, wl, send):
    group = lax.broadcasted_iota(jnp.int32, (CH, LANES), 1) // 16
    tiles = [
        [xv[pl.ds(c * (TILES * 128) + 2 * t + e, CH, stride=16), :] for t in range(8)]
        for e in range(2)
    ]

    def product(segments, table):
        hi, lo = split(
            jnp.concatenate(
                [
                    jnp.concatenate([tiles[e][s], tiles[e][(s + 1) % 8]], axis=1)
                    for e in range(2)
                    for s in segments
                ],
                axis=0,
            )
        )
        dot = functools.partial(jnp.dot, preferred_element_type=jnp.float32)
        spec = dot(hi, wh[table]) + dot(lo, wh[table]) + dot(hi, wl[table])
        re, im = spec[:, :LANES], spec[:, LANES:]
        amp = jnp.sqrt(re * re + im * im)
        n = len(segments)
        return [
            [amp[(e * n + s) * CH : (e * n + s + 1) * CH] for s in range(n)] for e in range(2)
        ]

    first, last = product(range(7), 0), product([7], 1)
    for e in range(2):
        v = first[e] + last[e]
        for d in (4, 2, 1):
            low = (group & d) == 0
            for i in range(8):
                if i & d == 0:
                    a, b = v[i], v[i + d]
                    v[i] = jnp.where(low, a, pltpu.roll(b, 16 * d, axis=1))
                    v[i + d] = jnp.where(low, pltpu.roll(a, LANES - 16 * d, axis=1), b)
        for b in range(8):
            send[c, b, e] = v[b]


def products_step(g, recv, taps, slot):
    lane = lax.broadcasted_iota(jnp.int32, (8, LANES), 1)

    def rows(xl, first):
        return recv[pl.ds((PX * g + xl + 1) * 16 + first, 8), :]

    centre = [[rows(x, first) for first in (1, 7)] for x in range(-1, PX + 1)]
    for x in range(PX):
        for half, first in enumerate((1, 7)):
            a = centre[x + 1][half]
            later = jnp.where(lane == 123, 0.0, pltpu.roll(a, LANES - 1, axis=1))
            earlier = jnp.where(lane == 124, 0.0, pltpu.roll(a, 1, axis=1))
            gt = later - earlier
            gi = rows(x, first + 1) - rows(x, first - 1)
            gx = centre[x + 2][half] - centre[x][half]
            for i, p in enumerate((gi * gt, gx * gt, gt * gt)):
                taps[slot, i, x, pl.ds(first - 1, 8), :] = p


def rows_step(g, taps, slot, q):
    w = side_weights()
    for x in range(PX):
        for i in range(3):
            tap = [taps[slot, i, x, pl.ds(k, 8), :] for k in range(7)]
            s = tap[3]
            for k in range(1, 4):
                s = s + w[k - 1] * (tap[3 - k] + tap[3 + k])
            q[i, pl.ds(pl.multiple_of((PX * g + x + 3) * 8, 8), 8), :] = s


def tensor_rows(recv, q, taps):
    last = 256 // PX - 1
    products_step(0, recv, taps, 0)

    def pair(h, carry):
        rows_step(2 * h, taps, 0, q)
        products_step(2 * h + 1, recv, taps, 1)
        rows_step(2 * h + 1, taps, 1, q)
        products_step(2 * h + 2, recv, taps, 0)
        return carry

    lax.fori_loop(0, last // 2, pair, 0)
    rows_step(last - 1, taps, 0, q)
    products_step(last, recv, taps, 1)
    rows_step(last, taps, 1, q)


def smooth_step(g, q, tmat, turn, out):
    w = side_weights()
    sm = []
    for i in range(3):
        load = lambda x: q[i, pl.ds(pl.multiple_of((GX * g + x) * 8, 8), GX * 8), :]
        s = load(3)
        for k in range(1, 4):
            s = s + w[k - 1] * (load(3 - k) + load(3 + k))
        sm.append(s)
    hi, lo = split(jnp.concatenate(sm, axis=0))
    t = jnp.dot(
        jnp.concatenate([hi, lo], axis=1), tmat[...], preferred_element_type=jnp.float32
    )
    t = t[:, :LANES] + t[:, LANES:]
    m = GX * 8
    inv = -1.0 / (t[2 * m :] + 4.0 * TINY)
    for i in range(2):
        d = t[i * m : (i + 1) * m] * inv
        for x in range(GX):
            turn[i, x // 8, pl.ds(x % 8, 8, stride=8), :] = d[8 * x : 8 * x + 8]
        for block in range(GX // 8):
            for row in range(8):
                place = pl.ds(pl.multiple_of(row * 256 + GX * g + 8 * block, 8), 8)
                out[i, place, :] = turn[i, block, pl.ds(8 * row, 8), :]


def clear_rim(q):
    for i in range(3):
        for start in (0, 259 * 8):
            q[i, pl.ds(start, 24), :] = jnp.zeros((24, LANES), jnp.float32)


def exchange_kernel(
    x_hbm, bins_hbm, dip, last, xv, bins_ref, wh, wl, send, recv, q, tmat, taps, turn, in_sem, ssem, rsem, own_sem
):
    band, tile = lax.axis_index("band"), lax.axis_index("tile")
    me = band * 32 + tile
    home = tile >> 2

    def partner(k):
        other = me ^ k
        return other >> 5, other & 31

    barrier = pltpu.get_barrier_semaphore()

    def greet(k, carry):
        pl.semaphore_signal(barrier, inc=1, device_id=partner(k), device_id_type=MESH)
        return carry

    load = pltpu.make_async_copy(x_hbm, xv.at[pl.ds(64, 4096)], in_sem.at[0])
    load.start()
    load_bins = pltpu.make_async_copy(bins_hbm, bins_ref, in_sem.at[1])
    load_bins.start()
    lax.fori_loop(1, 128, greet, 0)
    load_bins.wait()
    build_table(bins_ref, wh, wl)
    build_time_matrix(tmat)
    for start in (0, 4160):
        xv[pl.ds(start, 64), :] = jnp.zeros((64, LANES), jnp.float32)
    for start in (0, 257 * 16):
        recv[pl.ds(start, 16), :] = jnp.zeros((16, LANES), jnp.float32)
        last[pl.ds(start, 16), :] = jnp.zeros((16, LANES), jnp.float32)
    clear_rim(q)
    load.wait()

    def step_of(half, m):
        return (m << 1) | ((m ^ (m >> 1) ^ half) & 1)

    def form(half):
        def body(m, carry):
            amplitude_step(home ^ step_of(half, m), xv, wh, wl, send)
            return carry

        lax.fori_loop(0, 4, body, 0)

    def chunk(j, e, b2, t2):
        source = send.at[t2 >> 2, b2 * 2 + j, e, pl.ds(pl.multiple_of((t2 & 3) * 8, 8), 16)]
        place = pl.ds(pl.multiple_of((2 * me + e + 1) * 16, 16), 16)
        return source, (recv, last)[j].at[place]

    def push(j, k):
        b2, t2 = partner(k)
        for e in range(2):
            src, dst = chunk(j, e, b2, t2)
            pltpu.make_async_remote_copy(
                src, dst, ssem.at[j], rsem.at[j], device_id=(b2, t2), device_id_type=MESH
            ).start()

    def push_half(half):
        def body(n, carry):
            n = (n * 5) & 63
            push(0, ((n & 48) << 1) | (step_of(half, (n >> 2) & 3) << 2) | (n & 3))
            return carry

        lax.fori_loop(1 - half, 64, body, 0)

    def keep(j):
        own = []
        for e in range(2):
            src, dst = chunk(j, e, band, tile)
            own.append(pltpu.make_async_copy(src, dst, own_sem.at[j, e]))
            own[-1].start()
        return own

    form(0)
    pl.semaphore_wait(barrier, 127)
    own = keep(0)
    push_half(0)
    form(1)
    push_half(1)

    def arrivals(j):
        part = (recv, last)[j].at[pl.ds(16, 254 * 16)]
        return pltpu.make_async_remote_copy(
            part,
            part,
            ssem.at[j],
            rsem.at[j],
            device_id=(band, tile ^ 1),
            device_id_type=MESH,
        )

    def second(k, carry):
        push(1, (k * 83) & 127)
        return carry

    lax.fori_loop(1, 128, second, 0)
    own += keep(1)
    for copy in own[:2]:
        copy.wait()
    arrivals(0).wait_recv()

    def smooth(g, carry):
        smooth_step(g, q, tmat, turn, dip)
        return carry

    tensor_rows(recv, q, taps)
    lax.fori_loop(0, 256 // GX, smooth, 0)
    for copy in own[2:]:
        copy.wait()
    arrivals(1).wait_recv()
    for j in range(2):
        arrivals(j).wait_send()


def dips_kernel(dip, last, out_hbm, q, out, tmat, taps, turn, sems, osems):
    give = pltpu.make_async_copy(dip, out_hbm.at[0], sems.at[0])
    give.start()
    clear_rim(q)
    build_time_matrix(tmat)

    def result(i, g):
        return [
            pltpu.make_async_copy(
                out.at[i, pl.ds(pl.multiple_of(256 * row + GX * g, GX), GX)],
                out_hbm.at[1, i, pl.ds(pl.multiple_of(256 * row + GX * g, GX), GX)],
                osems.at[g],
            )
            for row in range(8)
        ]

    def smooth(g, carry):
        smooth_step(g, q, tmat, turn, out)
        for i in range(2):
            for copy in result(i, g):
                copy.start()
        return carry

    tensor_rows(last, q, taps)
    lax.fori_loop(0, 256 // GX, smooth, 0)

    def drain(g, carry):
        for i in range(2):
            pltpu.make_async_copy(
                out.at[i, pl.ds(0, 8 * GX)], out_hbm.at[1, i, pl.ds(0, 8 * GX)], osems.at[g]
            ).wait()
        return carry

    lax.fori_loop(0, 256 // GX, drain, 0)
    give.wait()


def local(traces, bins):
    x = traces.reshape(256, 2, 8, LANES).transpose(0, 2, 1, 3).reshape(4096, LANES)
    x = pltpu.with_memory_space_constraint(x, pltpu.HBM)
    bins = pltpu.with_memory_space_constraint(bins, pltpu.HBM)
    f32 = jnp.float32
    dma = pltpu.SemaphoreType.DMA
    anywhere = pl.BlockSpec(memory_space=pl.ANY)
    in_vmem = pl.BlockSpec(memory_space=pltpu.VMEM)
    field = pltpu.VMEM((2, 2048, LANES), f32)
    window = pltpu.VMEM((258 * 16, LANES), f32)
    tensor = pltpu.VMEM((3, 262 * 8, LANES), f32)
    matrix = pltpu.VMEM((2 * NF, 2 * NF), jnp.bfloat16)
    tap_rows = pltpu.VMEM((2, 3, PX, 16, LANES), f32)
    turned = pltpu.VMEM((2, GX // 8, 64, LANES), f32)
    dip, last = pl.pallas_call(
        exchange_kernel,
        out_shape=(
            jax.ShapeDtypeStruct((2, 2048, LANES), f32),
            jax.ShapeDtypeStruct((258 * 16, LANES), f32),
        ),
        in_specs=[pl.BlockSpec(memory_space=pltpu.HBM)] * 2,
        out_specs=(in_vmem, in_vmem),
        scratch_shapes=[
            pltpu.VMEM((264 * 16, LANES), f32),
            pltpu.SMEM((8,), jnp.int32),
            pltpu.VMEM((2, 256, 256), jnp.bfloat16),
            pltpu.VMEM((2, 256, 256), jnp.bfloat16),
            pltpu.VMEM((8, 8, 2, CH, LANES), f32),
            window,
            tensor,
            matrix,
            tap_rows,
            turned,
            dma((2,)),
            dma((2,)),
            dma((2,)),
            dma((2, 2)),
        ],
        compiler_params=pltpu.CompilerParams(
            collective_id=0, has_side_effects=True, vmem_limit_bytes=40 << 20
        ),
        name="transform_exchange",
    )(x, bins)
    out = pl.pallas_call(
        dips_kernel,
        out_shape=jax.ShapeDtypeStruct((2, 2, 2048, LANES), f32),
        in_specs=[in_vmem, in_vmem],
        out_specs=anywhere,
        scratch_shapes=[tensor, field, matrix, tap_rows, turned, dma((2,)), dma((8,))],
        compiler_params=pltpu.CompilerParams(vmem_limit_bytes=32 << 20),
        name="last_band_dips",
    )(dip, last)
    return out.reshape(2, 2, 8, 256, NF)


def solution(mesh):
    in_specs = (P(None, ("band", "tile"), None), P())
    out_specs = P("band", None, "tile", None, None)
    return jax.shard_map(local, mesh=mesh, in_specs=in_specs, out_specs=out_specs, check_vma=False)
```

```python
import functools
import math

import jax
import jax.numpy as jnp
from jax import lax
from jax.experimental import pallas as pl
from jax.experimental.pallas import tpu as pltpu
from jax.sharding import PartitionSpec as P

WIN = 64
R = 3
NF = 128
SIGMA = 2.0
TINY = 1e-6
MESH = pl.DeviceIdType.MESH
LANES = 128
TILES = 4
CH = 8 * TILES + 8
PX = 8
GX = 64


def smooth_weights():
    w = [math.exp(-(k * k) / (2.0 * SIGMA * SIGMA)) for k in range(-R, R + 1)]
    total = sum(w)
    return [v / total for v in w]


def side_weights():
    w = smooth_weights()
    return [w[R + k] / w[R] for k in range(1, R + 1)]


def split(x):
    hi = x.astype(jnp.bfloat16)
    return hi, (x - hi.astype(jnp.float32)).astype(jnp.bfloat16)


def build_time_matrix(tmat):
    lane = lax.broadcasted_iota(jnp.int32, (NF, NF), 0)
    frame = lax.broadcasted_iota(jnp.int32, (NF, NF), 1)
    away = jnp.abs(((lane + 4) & (NF - 1)) - frame)
    value = jnp.zeros((NF, NF), jnp.float32)
    w = smooth_weights()
    for k in range(R + 1):
        value = jnp.where(away == k, w[R + k] * w[R] * w[R], value)
    hi, lo = split(value)
    tmat[pl.ds(0, NF), pl.ds(0, NF)] = hi
    tmat[pl.ds(NF, NF), pl.ds(0, NF)] = hi
    tmat[pl.ds(0, NF), pl.ds(NF, NF)] = lo
    tmat[pl.ds(NF, NF), pl.ds(NF, NF)] = jnp.zeros((NF, NF), jnp.bfloat16)


def build_table(bins_ref, wh, wl):
    k = lax.broadcasted_iota(jnp.int32, (256, LANES), 0)
    lane = lax.broadcasted_iota(jnp.int32, (256, LANES), 1)
    group = lane // 16
    bins = jnp.zeros((256, LANES), jnp.int32)
    for b in range(8):
        bins = jnp.where(group == b, bins_ref[b], bins)
    frame = lane % 16
    n = k - 8 * frame
    inside = (n >= 0) & (n < WIN)
    step = 2.0 * math.pi / WIN
    taper = 0.5 - 0.5 * jnp.cos(step * n.astype(jnp.float32))
    angle = step * ((bins * n) & (WIN - 1)).astype(jnp.float32)
    re = jnp.where(inside, taper * jnp.cos(angle), 0.0)
    im = jnp.where(inside, -(taper * jnp.sin(angle)), 0.0)
    keep = (frame < 12) == (k < 128)
    for c, part in enumerate((re, im)):
        cols = slice(c * LANES, (c + 1) * LANES)
        for s, value in enumerate((part, jnp.where(keep, part, 0.0))):
            hi, lo = split(value)
            wh[s, :, cols] = hi
            wl[s, :, cols] = lo


def amplitude_step(c, xv, wh, wl, send):
    group = lax.broadcasted_iota(jnp.int32, (CH, LANES), 1) // 16
    tiles = [
        [xv[pl.ds(c * (TILES * 128) + 2 * t + e, CH, stride=16), :] for t in range(8)]
        for e in range(2)
    ]

    def product(segments, table):
        hi, lo = split(
            jnp.concatenate(
                [
                    jnp.concatenate([tiles[e][s], tiles[e][(s + 1) % 8]], axis=1)
                    for e in range(2)
                    for s in segments
                ],
                axis=0,
            )
        )
        dot = functools.partial(jnp.dot, preferred_element_type=jnp.float32)
        spec = dot(hi, wh[table]) + dot(lo, wh[table]) + dot(hi, wl[table])
        re, im = spec[:, :LANES], spec[:, LANES:]
        amp = jnp.sqrt(re * re + im * im)
        n = len(segments)
        return [
            [amp[(e * n + s) * CH : (e * n + s + 1) * CH] for s in range(n)] for e in range(2)
        ]

    first, last = product(range(7), 0), product([7], 1)
    for e in range(2):
        v = first[e] + last[e]
        for d in (4, 2, 1):
            low = (group & d) == 0
            for i in range(8):
                if i & d == 0:
                    a, b = v[i], v[i + d]
                    v[i] = jnp.where(low, a, pltpu.roll(b, 16 * d, axis=1))
                    v[i + d] = jnp.where(low, pltpu.roll(a, LANES - 16 * d, axis=1), b)
        for b in range(8):
            send[c, b, e] = v[b]


def products_step(g, recv, taps, slot):
    lane = lax.broadcasted_iota(jnp.int32, (8, LANES), 1)

    def rows(xl, first):
        return recv[pl.ds((PX * g + xl + 1) * 16 + first, 8), :]

    centre = [[rows(x, first) for first in (1, 7)] for x in range(-1, PX + 1)]
    for x in range(PX):
        for half, first in enumerate((1, 7)):
            a = centre[x + 1][half]
            later = jnp.where(lane == 123, 0.0, pltpu.roll(a, LANES - 1, axis=1))
            earlier = jnp.where(lane == 124, 0.0, pltpu.roll(a, 1, axis=1))
            gt = later - earlier
            gi = rows(x, first + 1) - rows(x, first - 1)
            gx = centre[x + 2][half] - centre[x][half]
            for i, p in enumerate((gi * gt, gx * gt, gt * gt)):
                taps[slot, i, x, pl.ds(first - 1, 8), :] = p


def rows_step(g, taps, slot, q):
    w = side_weights()
    for x in range(PX):
        for i in range(3):
            tap = [taps[slot, i, x, pl.ds(k, 8), :] for k in range(7)]
            s = tap[3]
            for k in range(1, 4):
                s = s + w[k - 1] * (tap[3 - k] + tap[3 + k])
            q[i, pl.ds(pl.multiple_of((PX * g + x + 3) * 8, 8), 8), :] = s


def tensor_rows(recv, q, taps):
    last = 256 // PX - 1
    products_step(0, recv, taps, 0)

    def pair(h, carry):
        rows_step(2 * h, taps, 0, q)
        products_step(2 * h + 1, recv, taps, 1)
        rows_step(2 * h + 1, taps, 1, q)
        products_step(2 * h + 2, recv, taps, 0)
        return carry

    lax.fori_loop(0, last // 2, pair, 0)
    rows_step(last - 1, taps, 0, q)
    products_step(last, recv, taps, 1)
    rows_step(last, taps, 1, q)


def smooth_step(g, q, tmat, turn, out):
    w = side_weights()
    sm = []
    for i in range(3):
        load = lambda x: q[i, pl.ds(pl.multiple_of((GX * g + x) * 8, 8), GX * 8), :]
        s = load(3)
        for k in range(1, 4):
            s = s + w[k - 1] * (load(3 - k) + load(3 + k))
        sm.append(s)
    hi, lo = split(jnp.concatenate(sm, axis=0))
    t = jnp.dot(
        jnp.concatenate([hi, lo], axis=1), tmat[...], preferred_element_type=jnp.float32
    )
    t = t[:, :LANES] + t[:, LANES:]
    m = GX * 8
    inv = -1.0 / (t[2 * m :] + 4.0 * TINY)
    for i in range(2):
        d = t[i * m : (i + 1) * m] * inv
        for x in range(GX):
            turn[i, x // 8, pl.ds(x % 8, 8, stride=8), :] = d[8 * x : 8 * x + 8]
        for block in range(GX // 8):
            for row in range(8):
                place = pl.ds(pl.multiple_of(row * 256 + GX * g + 8 * block, 8), 8)
                out[i, place, :] = turn[i, block, pl.ds(8 * row, 8), :]


def clear_rim(q):
    for i in range(3):
        for start in (0, 259 * 8):
            q[i, pl.ds(start, 24), :] = jnp.zeros((24, LANES), jnp.float32)


def exchange_kernel(
    x_hbm, bins_hbm, dip, last, xv, bins_ref, wh, wl, send, recv, q, tmat, taps, turn, in_sem, ssem, rsem, own_sem
):
    band, tile = lax.axis_index("band"), lax.axis_index("tile")
    me = band * 32 + tile
    home = tile >> 2

    def partner(k):
        other = me ^ k
        return other >> 5, other & 31

    barrier = pltpu.get_barrier_semaphore()

    def greet(k, carry):
        pl.semaphore_signal(barrier, inc=1, device_id=partner(k), device_id_type=MESH)
        return carry

    load = pltpu.make_async_copy(x_hbm, xv.at[pl.ds(64, 4096)], in_sem.at[0])
    load.start()
    load_bins = pltpu.make_async_copy(bins_hbm, bins_ref, in_sem.at[1])
    load_bins.start()
    lax.fori_loop(1, 128, greet, 0)
    load_bins.wait()
    build_table(bins_ref, wh, wl)
    build_time_matrix(tmat)
    for start in (0, 4160):
        xv[pl.ds(start, 64), :] = jnp.zeros((64, LANES), jnp.float32)
    for start in (0, 257 * 16):
        recv[pl.ds(start, 16), :] = jnp.zeros((16, LANES), jnp.float32)
        last[pl.ds(start, 16), :] = jnp.zeros((16, LANES), jnp.float32)
    clear_rim(q)
    load.wait()

    def step_of(half, m):
        return (m << 1) | ((m ^ (m >> 1) ^ half) & 1)

    def form(half):
        def body(m, carry):
            amplitude_step(home ^ step_of(half, m), xv, wh, wl, send)
            return carry

        lax.fori_loop(0, 4, body, 0)

    def chunk(j, e, b2, t2):
        source = send.at[t2 >> 2, b2 * 2 + j, e, pl.ds(pl.multiple_of((t2 & 3) * 8, 8), 16)]
        place = pl.ds(pl.multiple_of((2 * me + e + 1) * 16, 16), 16)
        return source, (recv, last)[j].at[place]

    def push(j, k):
        b2, t2 = partner(k)
        for e in range(2):
            src, dst = chunk(j, e, b2, t2)
            pltpu.make_async_remote_copy(
                src, dst, ssem.at[j], rsem.at[j], device_id=(b2, t2), device_id_type=MESH
            ).start()

    def push_half(half):
        def body(n, carry):
            n = (n * 5) & 63
            push(0, ((n & 48) << 1) | (step_of(half, (n >> 2) & 3) << 2) | (n & 3))
            return carry

        lax.fori_loop(1 - half, 64, body, 0)

    def keep(j):
        own = []
        for e in range(2):
            src, dst = chunk(j, e, band, tile)
            own.append(pltpu.make_async_copy(src, dst, own_sem.at[j, e]))
            own[-1].start()
        return own

    form(0)
    pl.semaphore_wait(barrier, 127)
    own = keep(0)
    push_half(0)
    form(1)
    push_half(1)

    def arrivals(j):
        part = (recv, last)[j].at[pl.ds(16, 254 * 16)]
        return pltpu.make_async_remote_copy(
            part,
            part,
            ssem.at[j],
            rsem.at[j],
            device_id=(band, tile ^ 1),
            device_id_type=MESH,
        )

    def second(k, carry):
        push(1, (k * 115) & 127)
        return carry

    lax.fori_loop(1, 128, second, 0)
    own += keep(1)
    for copy in own[:2]:
        copy.wait()
    arrivals(0).wait_recv()

    def smooth(g, carry):
        smooth_step(g, q, tmat, turn, dip)
        return carry

    tensor_rows(recv, q, taps)
    lax.fori_loop(0, 256 // GX, smooth, 0)
    for copy in own[2:]:
        copy.wait()
    arrivals(1).wait_recv()
    for j in range(2):
        arrivals(j).wait_send()


def dips_kernel(dip, last, out_hbm, q, out, tmat, taps, turn, sems, osems):
    give = pltpu.make_async_copy(dip, out_hbm.at[0], sems.at[0])
    give.start()
    clear_rim(q)
    build_time_matrix(tmat)

    def result(i, g):
        return [
            pltpu.make_async_copy(
                out.at[i, pl.ds(pl.multiple_of(256 * row + GX * g, GX), GX)],
                out_hbm.at[1, i, pl.ds(pl.multiple_of(256 * row + GX * g, GX), GX)],
                osems.at[g],
            )
            for row in range(8)
        ]

    def smooth(g, carry):
        smooth_step(g, q, tmat, turn, out)
        for i in range(2):
            for copy in result(i, g):
                copy.start()
        return carry

    tensor_rows(last, q, taps)
    lax.fori_loop(0, 256 // GX, smooth, 0)

    def drain(g, carry):
        for i in range(2):
            pltpu.make_async_copy(
                out.at[i, pl.ds(0, 8 * GX)], out_hbm.at[1, i, pl.ds(0, 8 * GX)], osems.at[g]
            ).wait()
        return carry

    lax.fori_loop(0, 256 // GX, drain, 0)
    give.wait()


def local(traces, bins):
    x = traces.reshape(256, 2, 8, LANES).transpose(0, 2, 1, 3).reshape(4096, LANES)
    x = pltpu.with_memory_space_constraint(x, pltpu.HBM)
    bins = pltpu.with_memory_space_constraint(bins, pltpu.HBM)
    f32 = jnp.float32
    dma = pltpu.SemaphoreType.DMA
    anywhere = pl.BlockSpec(memory_space=pl.ANY)
    in_vmem = pl.BlockSpec(memory_space=pltpu.VMEM)
    field = pltpu.VMEM((2, 2048, LANES), f32)
    window = pltpu.VMEM((258 * 16, LANES), f32)
    tensor = pltpu.VMEM((3, 262 * 8, LANES), f32)
    matrix = pltpu.VMEM((2 * NF, 2 * NF), jnp.bfloat16)
    tap_rows = pltpu.VMEM((2, 3, PX, 16, LANES), f32)
    turned = pltpu.VMEM((2, GX // 8, 64, LANES), f32)
    dip, last = pl.pallas_call(
        exchange_kernel,
        out_shape=(
            jax.ShapeDtypeStruct((2, 2048, LANES), f32),
            jax.ShapeDtypeStruct((258 * 16, LANES), f32),
        ),
        in_specs=[pl.BlockSpec(memory_space=pltpu.HBM)] * 2,
        out_specs=(in_vmem, in_vmem),
        scratch_shapes=[
            pltpu.VMEM((264 * 16, LANES), f32),
            pltpu.SMEM((8,), jnp.int32),
            pltpu.VMEM((2, 256, 256), jnp.bfloat16),
            pltpu.VMEM((2, 256, 256), jnp.bfloat16),
            pltpu.VMEM((8, 8, 2, CH, LANES), f32),
            window,
            tensor,
            matrix,
            tap_rows,
            turned,
            dma((2,)),
            dma((2,)),
            dma((2,)),
            dma((2, 2)),
        ],
        compiler_params=pltpu.CompilerParams(
            collective_id=0, has_side_effects=True, vmem_limit_bytes=40 << 20
        ),
        name="transform_exchange",
    )(x, bins)
    out = pl.pallas_call(
        dips_kernel,
        out_shape=jax.ShapeDtypeStruct((2, 2, 2048, LANES), f32),
        in_specs=[in_vmem, in_vmem],
        out_specs=anywhere,
        scratch_shapes=[tensor, field, matrix, tap_rows, turned, dma((2,)), dma((8,))],
        compiler_params=pltpu.CompilerParams(vmem_limit_bytes=32 << 20),
        name="last_band_dips",
    )(dip, last)
    return out.reshape(2, 2, 8, 256, NF)


def solution(mesh):
    in_specs = (P(None, ("band", "tile"), None), P())
    out_specs = P("band", None, "tile", None, None)
    return jax.shard_map(local, mesh=mesh, in_specs=in_specs, out_specs=out_specs, check_vma=False)
```
